32 devices in a mesh: section: 4 (over y, x), student: 2 (over core), dp: 4 (over z).
Axes of the slice: x: 2, y: 2, z: 4, core: 2. Of those that a mesh axis runs over, the one named last changes fastest.
Arguments:
- in_flight: bfloat16 [4, 2, 128, 4096], P('section', 'student'), may hold values from -6 to 6
- segments: int32 [4, 2, 128], P(None, 'student'), may hold values from 0 to 3, never falling along the last dimension, each value on 1 to 64 neighbouring positions
- norm_gain: float32 [4, 4096], P('section'), may hold values from 0.5 to 1.5
- w_qkv: bfloat16 [4, 4096, 3, 1024], P('section', None, None, 'dp')
- w_out: bfloat16 [4, 1024, 4096], P('section', 'dp'), may hold values from -0.1875 to 0.1875
- final_gain: float32 [4096], replicated, may hold values from 0.25 to 1.75
- student_rows: bfloat16 [2, 3, 2, 128, 1024], P('student', None, None, 'dp'), may hold values from -6 to 6
- student_gain: float32 [2, 1024], P('student'), may hold values from 0.5 to 1.5
- w_head: bfloat16 [2, 1024, 4096], P('student', None, 'section'), may hold values from -0.1875 to 0.1875
Outputs:
- advanced: bfloat16 [4, 2, 128, 4096], P('section', 'student', 'dp')
- grad_head: float32 [2, 1024, 4096], P('student', 'dp', 'section')
The draws below stay inside these ranges and needn't reach their ends.
Inputs may be any that keep to these rules, and one draw needn't show every extreme that they name: `segments`: along a micro-batch's tokens the crop numbers never fall; each of the 4 crops holds 1 to 64 tokens and one holds exactly 64.
All inputs are finite; a program needn't handle non-finite values.
Results may differ from the reference program's by a relative error of at most 0.025.
Values may be sent and summed in bfloat16 or wider, within the bound.
A program may use at most 64 MiB of HBM per device.

```python
import math
import jax
import jax.numpy as jnp
import numpy as np
from jax import lax

D = 4096
HEAD_SIZE = 128
SW = 1024
TOK = 128
TICKS = 3
CROPS = 4
CROP_MOST = 64
HEADS = 8
SECTIONS = 4
COLS = 2
GROUPS = 2
N_DP = 4


def draw_w_qkv(key, part):
    first = jax.random.fold_in(key, 11)
    width = HEADS * HEAD_SIZE
    base = jax.random.truncated_normal(first, -6.0, 6.0, (SECTIONS, D, 3, width), jnp.float32) * D ** (-0.5)
    return base.astype(jnp.bfloat16)


def raised(result, stream_key, source, target, blocks, factor):
    owner, partner = [(jnp.arange(result.shape[axis_at]) // (result.shape[axis_at] // blocks)).reshape([-1 if axis == axis_at else 1 for axis in range(result.ndim)]) for axis_at in (source, target)]
    chosen = jax.random.permutation(stream_key, blocks)[partner]
    strong = (owner == chosen) | (owner == (partner + blocks // 2) % blocks)
    return jnp.where(strong, factor * result, result)


def block_levels(own_key, extent, pieces, smallest, high):
    loudness, own = 1.0, jax.random.fold_in(own_key, 6)
    for axis_at, parts in pieces:
        heights = jnp.exp(jax.random.uniform(jax.random.fold_in(own, axis_at), (parts,), jnp.float32, smallest / len(pieces), high / len(pieces)))
        loudness = loudness * jnp.repeat(heights, extent[axis_at] // parts).reshape([-1 if axis == axis_at else 1 for axis in range(len(extent))])
    return loudness


def length_profile(amount, total, bound, lean):
    portions = [(1 << 20) // math.isqrt(standing ** lean) + 1 for standing in range(2, amount + 1)]
    spare, given = total - bound - (amount - 1), [1] * (amount - 1)
    while spare > 0:
        free = [i for i in range(amount - 1) if given[i] < bound]
        mass, budget = sum([portions[i] for i in free]), spare
        for i in free:
            extra = min(bound - given[i], max(1, budget * portions[i] // mass), spare)
            given[i] = given[i] + extra
            spare = spare - extra
    return np.array([bound] + given)


def ragged_sizes(stream_key, number_of, total, bound, skew):
    if number_of == 2:
        one = jax.random.randint(stream_key, (), max(1, total - bound), min(bound, total - 1) + 1)
        return jnp.stack([one, total - one])
    sizes = jnp.asarray(length_profile(number_of, total, bound, skew), jnp.int32)
    couples = (number_of - 1) // 2
    giver, receiver = sizes[1:1 + 2 * couples:2], sizes[2:2 + 2 * couples:2]
    margin = jnp.minimum(giver - 1, bound - receiver)
    moved = jax.random.randint(jax.random.fold_in(stream_key, 1), (couples,), 0, 1 << 20) % (margin + 1)
    sizes = sizes.at[1:1 + 2 * couples:2].set(giver - moved).at[2:2 + 2 * couples:2].set(receiver + moved)
    return sizes[jax.random.permutation(jax.random.fold_in(stream_key, 2), number_of)]


def normal_values(stream_key, dims, scale, most, shards=(), kind=jnp.bfloat16):
    entries = scale * jax.random.normal(stream_key, dims, jnp.float32)
    if shards:
        entries = entries * block_levels(stream_key, dims, shards, -0.22, 0.18)
    return jnp.clip(entries, -most, most).astype(kind)


def noise_with(rng, extent, scale, reach, shards, heavy, dtype=jnp.bfloat16):
    drawn = scale * jax.random.normal(rng, extent, jnp.float32)
    if shards:
        drawn = drawn * block_levels(rng, extent, shards, -0.22, 0.18)
    return jnp.clip(raised(drawn, jax.random.fold_in(rng, 3), *heavy), -reach, reach).astype(dtype)


def setup_inputs(seed: int = 0) -> dict:
    splits = jax.random.split(jax.random.key(seed), 10)
    return {
        "in_flight": normal_values(splits[0], (SECTIONS, COLS, TOK, D), 1.0, 6.0, ((0, 4), (1, 2))),
        "segments": jax.vmap(lambda own: jnp.searchsorted(jnp.cumsum(ragged_sizes(own, CROPS, TOK, CROP_MOST, 1)), jnp.arange(TOK), side="right"))(jax.random.split(splits[1], SECTIONS * COLS)).reshape((SECTIONS, COLS, TOK)).astype(jnp.int32),
        "norm_gain": jnp.clip(1.0 + 0.1 * jax.random.normal(splits[2], (SECTIONS, D), jnp.float32), 0.5, 1.5),
        "w_qkv": draw_w_qkv(jax.random.fold_in(splits[9], 71), 0),
        "w_out": normal_values(splits[4], (SECTIONS, HEADS * HEAD_SIZE, D), (HEADS * HEAD_SIZE) ** -0.5, 0.1875, ((0, 4), (1, 4))),
        "final_gain": jnp.clip(1.0 + 0.15 * jax.random.normal(splits[5], (D,), jnp.float32), 0.25, 1.75),
        "student_rows": noise_with(splits[6], (GROUPS, TICKS, COLS, TOK, SW), 1.0, 6.0, ((0, 2), (3, 4)), (3, 4, 4, 2.0)),
        "student_gain": jnp.clip(1.0 + 0.1 * jax.random.normal(splits[7], (GROUPS, SW), jnp.float32), 0.5, 1.5),
        "w_head": normal_values(splits[8], (GROUPS, SW, D), SW ** -0.5, 0.1875, ((0, 2), (2, 4))),
    }


def layer_norm(rows, gain):
    rows = rows.astype(jnp.float32)
    centred = rows - lax.optimization_barrier(jnp.mean(rows, axis=-1, keepdims=True))
    spread = lax.optimization_barrier(jnp.mean(centred * centred, axis=-1, keepdims=True))
    return centred * lax.rsqrt(spread + 1e-06) * gain.astype(jnp.float32)

def teacher_layer(state, crops, gain, weights_qkv, weights_out):
    tokens = state.shape[0]
    width = weights_out.shape[0]
    heads = width // HEAD_SIZE
    normed = layer_norm(state, gain).astype(jnp.bfloat16)
    qkv = jnp.dot(normed, weights_qkv.reshape(weights_qkv.shape[0], 3 * width), preferred_element_type=jnp.float32).astype(jnp.bfloat16)
    query = qkv[:, :width].reshape(tokens, heads, HEAD_SIZE).astype(jnp.float32)
    keys = qkv[:, width:2 * width].reshape(tokens, heads, HEAD_SIZE).astype(jnp.float32)
    values = qkv[:, 2 * width:].reshape(tokens, heads, HEAD_SIZE).astype(jnp.float32)
    scores = jnp.einsum('qhd,khd->hqk', query, keys) * HEAD_SIZE ** (-0.5)
    same = crops[:, None] == crops[None, :]
    scores = jnp.where(same[None], scores, -1e+30)
    top = lax.optimization_barrier(jnp.max(scores, axis=-1, keepdims=True))
    expo = jnp.exp(scores - top)
    probs = (expo / lax.optimization_barrier(jnp.sum(expo, axis=-1, keepdims=True))).astype(jnp.bfloat16)
    mixed = jnp.einsum('hqk,khd->qhd', probs.astype(jnp.float32), values).astype(jnp.bfloat16).reshape(tokens, width)
    part = width // N_DP
    partials = jnp.einsum('tjc,jcd->jtd', mixed.reshape(tokens, N_DP, part).astype(jnp.float32), weights_out.reshape(N_DP, part, -1).astype(jnp.float32))
    partials = lax.optimization_barrier(partials.astype(jnp.bfloat16)).astype(jnp.float32)
    return (state.astype(jnp.float32) + lax.optimization_barrier(jnp.sum(partials, axis=0))).astype(jnp.bfloat16)

def reference(in_flight, segments, norm_gain, w_qkv, w_out, final_gain, student_rows, student_gain, w_head):
    sections = in_flight.shape[0]
    layer = jax.vmap(teacher_layer, in_axes=(0, 0, None, None, None))
    advanced = jnp.zeros_like(in_flight)
    finished = [None] * TICKS
    for start in range(sections):
        state = in_flight[start]
        for tick in range(TICKS):
            where = start + tick
            if where < sections:
                state = layer(state, segments[start], norm_gain[where], w_qkv[where], w_out[where])
                if where == sections - 1:
                    finished[tick] = layer_norm(state, final_gain).astype(jnp.bfloat16)
        if start + TICKS < sections:
            advanced = advanced.at[start + TICKS].set(state)
    targets = jnp.stack(finished).astype(jnp.float32)
    share = TOK // N_DP
    grads = []
    for member in range(student_rows.shape[0]):
        feats = layer_norm(student_rows[member], student_gain[member]).astype(jnp.bfloat16)
        pred = jnp.einsum('tcns,sd->tcnd', feats.astype(jnp.float32), w_head[member].astype(jnp.float32))
        err = ((pred - targets) * (2.0 / TOK)).astype(jnp.bfloat16)
        feats_split = feats.reshape(TICKS, feats.shape[1], N_DP, share, SW)
        err_split = err.reshape(TICKS, err.shape[1], N_DP, share, D)

        def add_share(total, index):
            own_feats = lax.dynamic_index_in_dim(feats_split, index, 2, keepdims=False).reshape(-1, SW)
            own_err = lax.dynamic_index_in_dim(err_split, index, 2, keepdims=False).reshape(-1, D)
            term = jnp.dot(own_feats.T, own_err, preferred_element_type=jnp.float32).astype(jnp.bfloat16)
            term = lax.optimization_barrier(term).astype(jnp.float32)
            return (total + term, None)
        total, _ = lax.scan(add_share, jnp.zeros((SW, D), jnp.float32), jnp.arange(N_DP).astype(jnp.int32))
        grads.append(total)
    return (advanced, jnp.stack(grads))
```

```python
import functools

import jax
import jax.numpy as jnp
from jax import lax
from jax.experimental import pallas as pl
from jax.experimental.pallas import tpu as pltpu
from jax.sharding import PartitionSpec as P

HEAD_SIZE = 128
LN_ROWS = 16
BF16 = jnp.bfloat16
F32 = jnp.float32
MESH = pl.DeviceIdType.MESH


def layer_norm(rows, gain):
    rows = rows.astype(F32)
    centred = rows - jnp.mean(rows, axis=-1, keepdims=True)
    spread = jnp.mean(centred * centred, axis=-1, keepdims=True)
    return centred * lax.rsqrt(spread + 1e-06) * gain


def attend(query, keys, values, same):
    scores = lax.dot_general(
        query, keys, (((1,), (1,)), ((), ())), preferred_element_type=F32
    ) * HEAD_SIZE ** (-0.5)
    scores = jnp.where(same, scores, -1e30)
    top = jnp.max(scores, axis=-1, keepdims=True)
    expo = jnp.exp(scores - top)
    probs = (expo / jnp.sum(expo, axis=-1, keepdims=True)).astype(BF16)
    return jnp.dot(probs, values, preferred_element_type=F32).astype(BF16)


def window_kernel(
    S, M, Z, T, R,
    x_ref, seg_ref, gain_ref, wqkv_ref, wout_ref, fgain_ref, srows_ref, sgain_ref, whead_ref,
    adv_ref, grad_ref,
    wqkv, wofull, whead, normed, xfull, mixfull, xs, xrows, fin, tg, tbuf, advbuf,
    feats, pred, ffull, errfull,
    local_sem, wo_s, wo_r, wf_s, wf_r, mx_s, mx_r, sh_s, sh_r, ar_s, ar_r, al_s, al_r,
    ro_s, ro_r, ad_s, ad_r, tg_s, tg_r, fe_s, fe_r, er_s, er_r,
):
    s = lax.axis_index("section")
    c = lax.axis_index("student")
    z = lax.axis_index("dp")
    root = S - 1
    tokens, model = x_ref.shape
    wid = wout_ref.shape[0]
    share = tokens // Z
    cw = model // Z
    block = whead_ref.shape[1]
    sw = whead_ref.shape[0]
    fw = sw // Z
    step_rows = tokens // R
    halves = 2 if M % 2 == 0 else 1
    part = c % halves
    hw = wid // halves
    sends = []

    def remote(src, dst, send, recv, where):
        return pltpu.make_async_remote_copy(
            src_ref=src, dst_ref=dst, send_sem=send, recv_sem=recv,
            device_id=where, device_id_type=MESH,
        )

    def post(cond, build):
        if cond is True:
            build().start()
        else:
            pl.when(cond)(lambda: build().start())
        sends.append((cond, build))

    def zmod(value):
        return lax.rem(value + Z, Z)

    def cols(index):
        return pl.ds(pl.multiple_of(index * cw, 128), cw)

    load_qkv = pltpu.make_async_copy(wqkv_ref, wqkv, local_sem.at[0])
    load_head = pltpu.make_async_copy(whead_ref, whead, local_sem.at[1])
    own_wo = pltpu.make_async_copy(
        wout_ref.at[:, cols(z)],
        wofull.at[pl.ds(pl.multiple_of(z * wid, wid), wid), :],
        local_sem.at[2],
    )
    load_qkv.start()
    own_wo.start()
    load_head.start()

    barrier = pltpu.get_barrier_semaphore()

    def greet(where):
        pl.semaphore_signal(barrier, inc=1, device_id=where, device_id_type=MESH)

    for k in range(1, Z):
        greet((s, c, zmod(z + k)))
    for k in range(Z):
        pl.when(s > 0)(functools.partial(greet, (s - 1, c, zmod(z + k))))
        pl.when(s < root)(functools.partial(greet, (s + 1, c, zmod(z + k))))
    for at in range(S):
        far = jnp.logical_or(s - at > 1, at - s > 1)
        pl.when(far)(functools.partial(greet, (jnp.int32(at), c, z)))
        for dm in range(1, M):
            greet((jnp.int32(at), lax.rem(c + dm, M), z))
    for at in range(S):
        near = min(at, 1) + min(root - at, 1)
        peers = (Z - 1) + Z * near + (S - 1 - near) + S * (M - 1)
        pl.when(s == at)(functools.partial(pl.semaphore_wait, barrier, peers))

    def wo_rows(source, which):
        return pl.ds(pl.multiple_of(source * wid + which * hw, hw), hw)

    for k in sorted(range(1, Z), reverse=True):
        def build(k=k):
            to = zmod(z + k)
            return remote(
                wout_ref.at[pl.ds(pl.multiple_of(part * hw, hw), hw), cols(to)],
                wofull.at[wo_rows(z, part), :],
                wo_s.at[k - 1], wo_r.at[k - 1], (s, c, to),
            )
        post(True, build)

    def pass_on(k):
        source = zmod(z - k)
        mine = wofull.at[wo_rows(source, part), :]
        mate = c + 1 - 2 * part
        return remote(mine, mine, wf_s.at[k - 1], wf_r.at[k - 1], (s, mate, z))

    def gather_wo():
        for k in range(1, Z):
            source = zmod(z - k)
            mine = wofull.at[wo_rows(source, part), :]
            remote(mine, mine, wo_s.at[k - 1], wo_r.at[k - 1], (s, c, source)).wait_recv()
            if halves == 2:
                post(True, functools.partial(pass_on, k))
        if halves == 2:
            for k in range(1, Z):
                source = zmod(z - k)
                other = wofull.at[wo_rows(source, 1 - part), :]
                remote(other, other, wf_s.at[k - 1], wf_r.at[k - 1],
                       (s, c + 1 - 2 * part, z)).wait_recv()
        own_wo.wait()

    def student():
        rows = layer_norm(srows_ref[...].astype(F32).reshape(T * M * share, sw), sgain_ref[...])
        rows = rows.astype(BF16)
        for zz in range(Z):
            feats[zz] = rows[:, zz * fw:(zz + 1) * fw].reshape(T, M * share, fw)
        for k in range(1, Z):
            def build(k=k):
                to = zmod(z + k)
                return remote(feats.at[to], ffull.at[z], fe_s.at[k - 1], fe_r.at[k - 1], (s, c, to))
            post(True, build)
        ffull[z] = feats[z]
        load_head.wait()
        pred[...] = jnp.dot(rows, whead[...], preferred_element_type=F32).reshape(
            T, M, share, block
        )

    def errors(t):
        for cs in range(M):
            def take(cs=cs):
                there = tbuf.at[t, cs]
                remote(there, there, tg_s.at[t, 0], tg_r.at[t, cs], (root, cs, z)).wait_recv()
            pl.when(jnp.logical_or(s != root, c != cs))(take)
        err = (pred[t] - tbuf[t].astype(F32)) * (2.0 / tokens)
        errfull[t, z] = err.reshape(M * share, block).astype(BF16)
        for k in range(1, Z):
            def build(k=k):
                own = errfull.at[t, z]
                return remote(own, own, er_s.at[t, k - 1], er_r.at[t, k - 1],
                              (s, c, zmod(z + k)))
            post(True, build)

    def gradient(t):
        for k in range(1, Z):
            there = errfull.at[t, zmod(z - k)]
            remote(there, there, er_s.at[t, k - 1], er_r.at[t, k - 1],
                   (s, c, zmod(z - k))).wait_recv()
        term = lax.dot_general(
            ffull[:, t].reshape(Z * M * share, fw), errfull[t].reshape(Z * M * share, block),
            (((0,), (0,)), ((), ())), preferred_element_type=F32,
        )
        if t == 0:
            grad_ref[...] = term
        else:
            grad_ref[...] += term

    def take_feats():
        for k in range(1, Z):
            there = ffull.at[zmod(z - k)]
            remote(there, there, fe_s.at[k - 1], fe_r.at[k - 1], (s, c, zmod(z - k))).wait_recv()

    def gather_state(t, active):
        def piece(r, origin):
            return xfull.at[t - 1, pl.ds(r * step_rows, step_rows), cols(origin)]

        def to_right(r, k):
            there = piece(r, z - k)
            return remote(there, there, ar_s.at[t - 1, k, r], ar_r.at[t - 1, k, r], (s, c, z + 1))

        def to_left(r, k):
            there = piece(r, z + k)
            return remote(there, there, al_s.at[t - 1, k, r], al_r.at[t - 1, k, r], (s, c, z - 1))

        def right_from(r, k):
            there = piece(r, z - k)
            remote(there, there, ar_s.at[t - 1, k - 1, r], ar_r.at[t - 1, k - 1, r],
                   (s, c, z - 1)).wait_recv()

        def left_from(r, k):
            there = piece(r, z + k)
            remote(there, there, al_s.at[t - 1, k - 1, r], al_r.at[t - 1, k - 1, r],
                   (s, c, z + 1)).wait_recv()

        for r in range(R):
            def first(r=r):
                there = piece(r, z)
                remote(there, there, sh_s.at[t - 1, r], sh_r.at[t - 1, r],
                       (s - 1, c, z)).wait_recv()
            pl.when(active)(first)
            post(jnp.logical_and(active, z < Z - 1), functools.partial(to_right, r, 0))
            post(jnp.logical_and(active, z > 0), functools.partial(to_left, r, 0))
        for k in range(1, Z):
            for r in range(R):
                pl.when(jnp.logical_and(active, z >= k))(functools.partial(right_from, r, k))
                if k < Z - 1:
                    post(jnp.logical_and(active, jnp.logical_and(z >= k, z < Z - 1)),
                         functools.partial(to_right, r, k))
                pl.when(jnp.logical_and(active, z + k < Z))(functools.partial(left_from, r, k))
                if k < Z - 1:
                    post(jnp.logical_and(active, jnp.logical_and(z + k < Z, z > 0)),
                         functools.partial(to_left, r, k))

    def mix_cols(index):
        return pl.ds(pl.multiple_of(index * wid, 128), wid)

    def mixing(t):
        source = x_ref if t == 0 else xfull.at[t - 1]

        def norm_rows(i, carry):
            rows = pl.ds(pl.multiple_of(i * LN_ROWS, LN_ROWS), LN_ROWS)
            normed[rows, :] = layer_norm(source[rows, :], gain_ref[...]).astype(BF16)
            return carry

        lax.fori_loop(0, tokens // LN_ROWS, norm_rows, 0)
        if t == 0:
            load_qkv.wait()
        rows = normed[...]
        query, keys, values = [
            jnp.dot(rows, wqkv[:, j * wid:(j + 1) * wid], preferred_element_type=F32).astype(BF16)
            for j in range(3)
        ]
        crops = jnp.broadcast_to(seg_ref[s - t].astype(F32), (tokens, tokens))
        same = crops == crops.T
        outs = []
        for h in range(wid // HEAD_SIZE):
            at = slice(h * HEAD_SIZE, (h + 1) * HEAD_SIZE)
            outs.append(attend(query[:, at], keys[:, at], values[:, at], same))
        mixfull[t, :, mix_cols(z)] = jnp.concatenate(outs, axis=1)

    def send_mixed(t, active):
        for k in range(1, Z):
            def build(k=k):
                own = mixfull.at[t, :, mix_cols(z)]
                return remote(own, own, mx_s.at[t, k - 1], mx_r.at[t, k - 1],
                              (s, c, zmod(z + k)))
            post(active, build)

    def project(t):
        for k in range(1, Z):
            there = mixfull.at[t, :, mix_cols(zmod(z - k))]
            remote(there, there, mx_s.at[t, k - 1], mx_r.at[t, k - 1],
                   (s, c, zmod(z - k))).wait_recv()
        own = x_ref[:, cols(z)] if t == 0 else xfull[t - 1, :, cols(z)]
        summed = own.astype(F32) + jnp.dot(mixfull[t], wofull[...], preferred_element_type=F32)
        if t < T - 1:
            xs[t] = summed.astype(BF16)
        xrows[t] = summed.reshape(Z, share, cw).astype(BF16)

    def send_state(t, active):
        if t < T - 1:
            for r in range(R):
                def build(r=r):
                    at = pl.ds(r * step_rows, step_rows)
                    return remote(xs.at[t, at, :], xfull.at[t, at, cols(z)],
                                  sh_s.at[t, r], sh_r.at[t, r], (s + 1, c, z))
                post(jnp.logical_and(active, s < root), build)
        else:
            for k in range(Z):
                def build(k=k):
                    to = zmod(z + k)
                    return remote(xrows.at[t, to], advbuf.at[:, cols(z)],
                                  ad_s.at[k], ad_r.at[k], (s + 1, c, to))
                post(jnp.logical_and(active, s < root), build)
        for k in range(1, Z):
            def build_row(k=k):
                to = zmod(z + k)
                return remote(xrows.at[t, to], fin.at[t, :, cols(z)],
                              ro_s.at[t, k - 1], ro_r.at[t, k - 1], (s, c, to))
            post(s == root, build_row)

    def finish(t):
        def rows():
            fin[t, :, cols(z)] = xrows[t, z]
            for k in range(1, Z):
                there = fin.at[t, :, cols(zmod(z - k))]
                remote(there, there, ro_s.at[t, k - 1], ro_r.at[t, k - 1],
                       (s, c, zmod(z - k))).wait_recv()
            tg[t] = layer_norm(fin[t], fgain_ref[...]).astype(BF16)
            tbuf[t, c] = tg[t, :, root * block:(root + 1) * block]

        pl.when(s == root)(rows)
        for to in range(S):
            for dm in range(M):
                if to == root and dm == 0:
                    continue

                def build(to=to, dm=dm):
                    return remote(
                        tg.at[t, :, to * block:(to + 1) * block], tbuf.at[t, c],
                        tg_s.at[t, to * M + dm], tg_r.at[t, c],
                        (jnp.int32(to), lax.rem(c + dm, M), z),
                    )
                post(s == root, build)

    for t in range(T):
        active = True if t == 0 else s >= t
        if t == 0:
            mixing(0)
        else:
            gather_state(t, active)
            pl.when(active)(functools.partial(mixing, t))
        send_mixed(t, active)
        if t == 0:
            student()
            gather_wo()
            project(0)
        else:
            errors(t - 1)
            pl.when(active)(functools.partial(project, t))
        send_state(t, active)
        finish(t)

    take_feats()
    for t in range(T - 1):
        gradient(t)
    errors(T - 1)
    gradient(T - 1)

    def arrived():
        for k in range(Z):
            there = advbuf.at[:, cols(zmod(z - k))]
            remote(there, there, ad_s.at[k], ad_r.at[k], (s - 1, c, zmod(z - k))).wait_recv()
        adv_ref[...] = advbuf[...]

    def nothing():
        adv_ref[...] = jnp.zeros_like(adv_ref)

    pl.when(s >= T)(arrived)
    pl.when(s < T)(nothing)
    for cond, build in sends:
        if cond is True:
            build().wait_send()
        else:
            pl.when(cond)(lambda build=build: build().wait_send())


def solution(mesh):
    S, M, Z = mesh.shape["section"], mesh.shape["student"], mesh.shape["dp"]

    def on_device(
        in_flight, segments, norm_gain, w_qkv, w_out, final_gain, student_rows, student_gain, w_head
    ):
        tokens, model = in_flight.shape[2:]
        wid = w_out.shape[1]
        T, share = student_rows.shape[1], tokens // Z
        sw, block = w_head.shape[1:]
        cw, fw = model // Z, sw // Z
        R = 4 if Z <= 4 else 2
        vmem = pl.BlockSpec(memory_space=pltpu.VMEM)
        hbm = pl.BlockSpec(memory_space=pl.ANY)
        dma = pltpu.SemaphoreType.DMA
        K = max(Z - 1, 1)
        adv, grad = pl.pallas_call(
            functools.partial(window_kernel, S, M, Z, T, R),
            out_shape=(
                jax.ShapeDtypeStruct((share, model), BF16),
                jax.ShapeDtypeStruct((fw, block), F32),
            ),
            in_specs=[vmem, vmem, vmem, hbm, hbm, vmem, vmem, vmem, hbm],
            out_specs=(vmem, vmem),
            scratch_shapes=[
                pltpu.VMEM((model, 3 * wid), BF16),
                pltpu.VMEM((Z * wid, cw), BF16),
                pltpu.VMEM((sw, block), BF16),
                pltpu.VMEM((tokens, model), BF16),
                pltpu.VMEM((T - 1, tokens, model), BF16),
                pltpu.VMEM((T, tokens, Z * wid), BF16),
                pltpu.VMEM((T - 1, tokens, cw), BF16),
                pltpu.VMEM((T, Z, share, cw), BF16),
                pltpu.VMEM((T, share, model), BF16),
                pltpu.VMEM((T, share, model), BF16),
                pltpu.VMEM((T, M, share, block), BF16),
                pltpu.VMEM((share, model), BF16),
                pltpu.VMEM((Z, T, M * share, fw), BF16),
                pltpu.VMEM((T, M, share, block), F32),
                pltpu.VMEM((Z, T, M * share, fw), BF16),
                pltpu.VMEM((T, Z, M * share, block), BF16),
                dma((3,)),
                dma((K,)), dma((K,)), dma((K,)), dma((K,)),
                dma((T, K)), dma((T, K)),
                dma((T - 1, R)), dma((T - 1, R)),
                dma((T - 1, K, R)), dma((T - 1, K, R)),
                dma((T - 1, K, R)), dma((T - 1, K, R)),
                dma((T, K)), dma((T, K)),
                dma((Z,)), dma((Z,)),
                dma((T, S * M)), dma((T, M)),
                dma((K,)), dma((K,)),
                dma((T, K)), dma((T, K)),
            ],
            compiler_params=pltpu.CompilerParams(
                collective_id=0, has_side_effects=True, vmem_limit_bytes=58 << 20
            ),
        )(
            in_flight[0, 0], segments, norm_gain, w_qkv[0].reshape(model, -1), w_out[0],
            final_gain[None], student_rows[0], student_gain, w_head[0],
        )
        return adv[None, None], grad[None]

    in_specs = (
        P("section", "student", None, None),
        P(None, "student", None),
        P("section", None),
        P("section", None, None, "dp"),
        P("section", "dp", None),
        P(),
        P("student", None, None, "dp", None),
        P("student", None),
        P("student", None, "section"),
    )
    out_specs = (P("section", "student", "dp", None), P("student", "dp", "section"))
    return jax.shard_map(
        on_device, mesh=mesh, in_specs=in_specs, out_specs=out_specs, check_vma=False
    )
```

```python
import functools

import jax
import jax.numpy as jnp
from jax import lax
from jax.experimental import pallas as pl
from jax.experimental.pallas import tpu as pltpu
from jax.sharding import PartitionSpec as P

HEAD_SIZE = 128
LN_ROWS = 16
BF16 = jnp.bfloat16
F32 = jnp.float32
MESH = pl.DeviceIdType.MESH


def layer_norm(rows, gain):
    rows = rows.astype(F32)
    centred = rows - jnp.mean(rows, axis=-1, keepdims=True)
    spread = jnp.mean(centred * centred, axis=-1, keepdims=True)
    return centred * lax.rsqrt(spread + 1e-06) * gain


def attend(query, keys, values, same):
    scores = lax.dot_general(
        query, keys, (((1,), (1,)), ((), ())), preferred_element_type=F32
    ) * HEAD_SIZE ** (-0.5)
    scores = jnp.where(same, scores, -1e30)
    top = jnp.max(scores, axis=-1, keepdims=True)
    expo = jnp.exp(scores - top)
    probs = (expo / jnp.sum(expo, axis=-1, keepdims=True)).astype(BF16)
    return jnp.dot(probs, values, preferred_element_type=F32).astype(BF16)


def window_kernel(
    S, M, Z, T, R,
    x_ref, seg_ref, gain_ref, wqkv_ref, wout_ref, fgain_ref, srows_ref, sgain_ref, whead_ref,
    adv_ref, grad_ref,
    wqkv, wofull, whead, normed, xfull, mixfull, xs, xrows, fin, tg, tbuf, advbuf,
    sall, pred, fown, errs,
    local_sem, wo_s, wo_r, wf_s, wf_r, mx_s, mx_r, sh_s, sh_r, ar_s, ar_r, al_s, al_r,
    ro_s, ro_r, ad_s, ad_r, tg_s, tg_r, fe_s, fe_r, fp_s, fp_r,
    er_s, er_r, ml_s, ml_r,
):
    s = lax.axis_index("section")
    c = lax.axis_index("student")
    z = lax.axis_index("dp")
    root = S - 1
    tokens, model = x_ref.shape
    wid = wout_ref.shape[0]
    share = tokens // Z
    cw = model // Z
    block = whead_ref.shape[1]
    sw = whead_ref.shape[0]
    fw = sw // Z
    ow = sw // S
    step_rows = tokens // R
    halves = 2 if M % 2 == 0 else 1
    part = c % halves
    hw = wid // halves
    sends = []

    def remote(src, dst, send, recv, where):
        return pltpu.make_async_remote_copy(
            src_ref=src, dst_ref=dst, send_sem=send, recv_sem=recv,
            device_id=where, device_id_type=MESH,
        )

    def post(cond, build):
        if cond is True:
            build().start()
        else:
            pl.when(cond)(lambda: build().start())
        sends.append((cond, build))

    def zmod(value):
        return lax.rem(value + Z, Z)

    def cols(index):
        return pl.ds(pl.multiple_of(index * cw, 128), cw)

    load_qkv = pltpu.make_async_copy(wqkv_ref, wqkv, local_sem.at[0])
    load_head = pltpu.make_async_copy(whead_ref, whead, local_sem.at[1])
    own_wo = pltpu.make_async_copy(
        wout_ref.at[:, cols(z)],
        wofull.at[pl.ds(pl.multiple_of(z * wid, wid), wid), :],
        local_sem.at[2],
    )
    load_qkv.start()
    own_wo.start()
    load_head.start()

    barrier = pltpu.get_barrier_semaphore()

    def greet(where):
        pl.semaphore_signal(barrier, inc=1, device_id=where, device_id_type=MESH)

    for k in range(1, Z):
        greet((s, c, zmod(z + k)))
    for k in range(Z):
        pl.when(s > 0)(functools.partial(greet, (s - 1, c, zmod(z + k))))
        pl.when(s < root)(functools.partial(greet, (s + 1, c, zmod(z + k))))
    for at in range(S):
        far = jnp.logical_or(s - at > 1, at - s > 1)
        pl.when(far)(functools.partial(greet, (jnp.int32(at), c, z)))
        for dm in range(1, M):
            greet((jnp.int32(at), lax.rem(c + dm, M), z))
    for at in range(S):
        near = min(at, 1) + min(root - at, 1)
        peers = (Z - 1) + Z * near + (S - 1 - near) + S * (M - 1)
        pl.when(s == at)(functools.partial(pl.semaphore_wait, barrier, peers))

    def wo_rows(source, which):
        return pl.ds(pl.multiple_of(source * wid + which * hw, hw), hw)

    for k in sorted(range(1, Z), reverse=True):
        def build(k=k):
            to = zmod(z + k)
            return remote(
                wout_ref.at[pl.ds(pl.multiple_of(part * hw, hw), hw), cols(to)],
                wofull.at[wo_rows(z, part), :],
                wo_s.at[k - 1], wo_r.at[k - 1], (s, c, to),
            )
        post(True, build)

    def pass_on(k):
        source = zmod(z - k)
        mine = wofull.at[wo_rows(source, part), :]
        mate = c + 1 - 2 * part
        return remote(mine, mine, wf_s.at[k - 1], wf_r.at[k - 1], (s, mate, z))

    def gather_wo():
        for k in range(1, Z):
            source = zmod(z - k)
            mine = wofull.at[wo_rows(source, part), :]
            remote(mine, mine, wo_s.at[k - 1], wo_r.at[k - 1], (s, c, source)).wait_recv()
            if halves == 2:
                post(True, functools.partial(pass_on, k))
        if halves == 2:
            for k in range(1, Z):
                source = zmod(z - k)
                other = wofull.at[wo_rows(source, 1 - part), :]
                remote(other, other, wf_s.at[k - 1], wf_r.at[k - 1],
                       (s, c + 1 - 2 * part, z)).wait_recv()
        own_wo.wait()

    def scols(index):
        return pl.ds(pl.multiple_of(index * ow, 128), ow)

    def spread_rows():
        sall[0] = srows_ref[...]
        for k in range(1, Z):
            def build(k=k):
                return remote(srows_ref.at[:, :, :, scols(s)], sall.at[k, :, :, :, scols(s)],
                              fe_s.at[k - 1], fe_r.at[k - 1], (s, c, zmod(z + k)))
            post(True, build)

    def pass_rows():
        for k in range(1, Z):
            there = sall.at[k, :, :, :, scols(s)]
            remote(there, there, fe_s.at[k - 1], fe_r.at[k - 1], (s, c, zmod(z - k))).wait_recv()
        for k in range(1, S):
            def build(k=k):
                there = sall.at[pl.ds(1, Z - 1), :, :, :, scols(s)]
                return remote(there, there, fp_s.at[k - 1], fp_r.at[k - 1],
                              (lax.rem(s + k, S), c, z))
            post(True, build)

    def student():
        for k in range(1, S):
            where = lax.rem(s + S - k, S)
            there = sall.at[pl.ds(1, Z - 1), :, :, :, scols(where)]
            remote(there, there, fp_s.at[k - 1], fp_r.at[k - 1], (where, c, z)).wait_recv()
        load_head.wait()

        def one(k, carry):
            rows = layer_norm(sall[k].astype(F32).reshape(T * M * share, sw), sgain_ref[...])
            rows = rows.astype(BF16)
            for zz in range(Z):
                def own(zz=zz):
                    fown[k] = rows[:, zz * fw:(zz + 1) * fw].reshape(T, M * share, fw)
                pl.when(z == zz)(own)
            pred[k] = jnp.dot(rows, whead[...], preferred_element_type=F32).reshape(
                T, M, share, block
            )
            return carry

        lax.fori_loop(0, Z, one, 0)

    def spread(t):
        def take():
            there = tbuf.at[t, c, 0]
            remote(there, there, tg_s.at[t, 0], tg_r.at[t], (root, c, z)).wait_recv()
        pl.when(s != root)(take)
        for k in range(1, Z):
            def build(k=k):
                return remote(tbuf.at[t, c, 0], tbuf.at[t, c, k], er_s.at[t, k - 1],
                              er_r.at[t, k - 1], (s, c, zmod(z + k)))
            post(True, build)

    def relay(t):
        for k in range(Z):
            there = tbuf.at[t, c, k]
            if k:
                remote(there, there, er_s.at[t, k - 1], er_r.at[t, k - 1],
                       (s, c, zmod(z - k))).wait_recv()
            for dm in range(1, M):
                def build(k=k, dm=dm):
                    there = tbuf.at[t, c, k]
                    return remote(there, there, ml_s.at[t, dm - 1, k], ml_r.at[t, dm - 1, k],
                                  (s, lax.rem(c + dm, M), z))
                post(True, build)

    def gradient(t):
        for dm in range(1, M):
            for k in range(Z):
                who = lax.rem(c + M - dm, M)
                there = tbuf.at[t, who, k]
                remote(there, there, ml_s.at[t, dm - 1, k], ml_r.at[t, dm - 1, k],
                       (s, who, z)).wait_recv()

        def one(k, carry):
            err = (pred[k, t] - tbuf[t, :, k].astype(F32)) * (2.0 / tokens)
            errs[k] = err.reshape(M * share, block).astype(BF16)
            return carry

        lax.fori_loop(0, Z, one, 0)
        term = lax.dot_general(
            fown[:, t].reshape(Z * M * share, fw), errs[...].reshape(Z * M * share, block),
            (((0,), (0,)), ((), ())), preferred_element_type=F32,
        )
        if t == 0:
            grad_ref[...] = term
        else:
            grad_ref[...] += term

    def gather_state(t, active):
        def piece(r, origin):
            return xfull.at[t - 1, pl.ds(r * step_rows, step_rows), cols(origin)]

        def to_right(r, k):
            there = piece(r, z - k)
            return remote(there, there, ar_s.at[t - 1, k, r], ar_r.at[t - 1, k, r], (s, c, z + 1))

        def to_left(r, k):
            there = piece(r, z + k)
            return remote(there, there, al_s.at[t - 1, k, r], al_r.at[t - 1, k, r], (s, c, z - 1))

        def right_from(r, k):
            there = piece(r, z - k)
            remote(there, there, ar_s.at[t - 1, k - 1, r], ar_r.at[t - 1, k - 1, r],
                   (s, c, z - 1)).wait_recv()

        def left_from(r, k):
            there = piece(r, z + k)
            remote(there, there, al_s.at[t - 1, k - 1, r], al_r.at[t - 1, k - 1, r],
                   (s, c, z + 1)).wait_recv()

        for r in range(R):
            def first(r=r):
                there = piece(r, z)
                remote(there, there, sh_s.at[t - 1, r], sh_r.at[t - 1, r],
                       (s - 1, c, z)).wait_recv()
            pl.when(active)(first)
            post(jnp.logical_and(active, z < Z - 1), functools.partial(to_right, r, 0))
            post(jnp.logical_and(active, z > 0), functools.partial(to_left, r, 0))
        for k in range(1, Z):
            for r in range(R):
                pl.when(jnp.logical_and(active, z >= k))(functools.partial(right_from, r, k))
                if k < Z - 1:
                    post(jnp.logical_and(active, jnp.logical_and(z >= k, z < Z - 1)),
                         functools.partial(to_right, r, k))
                pl.when(jnp.logical_and(active, z + k < Z))(functools.partial(left_from, r, k))
                if k < Z - 1:
                    post(jnp.logical_and(active, jnp.logical_and(z + k < Z, z > 0)),
                         functools.partial(to_left, r, k))

    def mix_cols(index):
        return pl.ds(pl.multiple_of(index * wid, 128), wid)

    def mixing(t):
        source = x_ref if t == 0 else xfull.at[t - 1]

        def norm_rows(i, carry):
            rows = pl.ds(pl.multiple_of(i * LN_ROWS, LN_ROWS), LN_ROWS)
            normed[rows, :] = layer_norm(source[rows, :], gain_ref[...]).astype(BF16)
            return carry

        lax.fori_loop(0, tokens // LN_ROWS, norm_rows, 0)
        if t == 0:
            load_qkv.wait()
        rows = normed[...]
        query, keys, values = [
            jnp.dot(rows, wqkv[j], preferred_element_type=F32).astype(BF16)
            for j in range(3)
        ]
        crops = jnp.broadcast_to(seg_ref[s - t].astype(F32), (tokens, tokens))
        same = crops == crops.T
        outs = []
        for h in range(wid // HEAD_SIZE):
            at = slice(h * HEAD_SIZE, (h + 1) * HEAD_SIZE)
            outs.append(attend(query[:, at], keys[:, at], values[:, at], same))
        mixfull[t, :, mix_cols(z)] = jnp.concatenate(outs, axis=1)

    def send_mixed(t, active):
        for k in range(1, Z):
            def build(k=k):
                own = mixfull.at[t, :, mix_cols(z)]
                return remote(own, own, mx_s.at[t, k - 1], mx_r.at[t, k - 1],
                              (s, c, zmod(z + k)))
            post(active, build)

    def project(t):
        for k in range(1, Z):
            there = mixfull.at[t, :, mix_cols(zmod(z - k))]
            remote(there, there, mx_s.at[t, k - 1], mx_r.at[t, k - 1],
                   (s, c, zmod(z - k))).wait_recv()
        own = x_ref[:, cols(z)] if t == 0 else xfull[t - 1, :, cols(z)]
        summed = own.astype(F32) + jnp.dot(mixfull[t], wofull[...], preferred_element_type=F32)
        if t < T - 1:
            xs[t] = summed.astype(BF16)
        xrows[t] = summed.reshape(Z, share, cw).astype(BF16)

    def send_state(t, active):
        if t < T - 1:
            for r in range(R):
                def build(r=r):
                    at = pl.ds(r * step_rows, step_rows)
                    return remote(xs.at[t, at, :], xfull.at[t, at, cols(z)],
                                  sh_s.at[t, r], sh_r.at[t, r], (s + 1, c, z))
                post(jnp.logical_and(active, s < root), build)
        else:
            for k in range(Z):
                def build(k=k):
                    to = zmod(z + k)
                    return remote(xrows.at[t, to], advbuf.at[:, cols(z)],
                                  ad_s.at[k], ad_r.at[k], (s + 1, c, to))
                post(jnp.logical_and(active, s < root), build)
        for k in range(1, Z):
            def build_row(k=k):
                to = zmod(z + k)
                return remote(xrows.at[t, to], fin.at[t, :, cols(z)],
                              ro_s.at[t, k - 1], ro_r.at[t, k - 1], (s, c, to))
            post(s == root, build_row)

    def finish(t):
        def rows():
            fin[t, :, cols(z)] = xrows[t, z]
            for k in range(1, Z):
                there = fin.at[t, :, cols(zmod(z - k))]
                remote(there, there, ro_s.at[t, k - 1], ro_r.at[t, k - 1],
                       (s, c, zmod(z - k))).wait_recv()
            tg[t] = layer_norm(fin[t], fgain_ref[...]).astype(BF16)
            tbuf[t, c, 0] = tg[t, :, root * block:(root + 1) * block]

        pl.when(s == root)(rows)
        for to in range(root):
            def build(to=to):
                return remote(tg.at[t, :, to * block:(to + 1) * block], tbuf.at[t, c, 0],
                              tg_s.at[t, to], tg_r.at[t], (jnp.int32(to), c, z))
            post(s == root, build)

    for t in range(T):
        active = True if t == 0 else s >= t
        if t == 0:
            mixing(0)
        else:
            gather_state(t, active)
            if t == 1:
                pass_rows()
            else:
                relay(t - 2)
                spread(t - 1)
            pl.when(active)(functools.partial(mixing, t))
        send_mixed(t, active)
        if t == 0:
            spread_rows()
            gather_wo()
            project(0)
        else:
            if t == 1:
                spread(0)
            if t == T - 1:
                relay(t - 1)
                student()
            pl.when(active)(functools.partial(project, t))
        send_state(t, active)
        if t == T - 1:
            for before in range(t):
                gradient(before)
        finish(t)

    spread(T - 1)
    relay(T - 1)
    gradient(T - 1)

    def arrived():
        for k in range(Z):
            there = advbuf.at[:, cols(zmod(z - k))]
            remote(there, there, ad_s.at[k], ad_r.at[k], (s - 1, c, zmod(z - k))).wait_recv()
        adv_ref[...] = advbuf[...]

    def nothing():
        adv_ref[...] = jnp.zeros_like(adv_ref)

    pl.when(s >= T)(arrived)
    pl.when(s < T)(nothing)
    for cond, build in sends:
        if cond is True:
            build().wait_send()
        else:
            pl.when(cond)(lambda build=build: build().wait_send())


def solution(mesh):
    S, M, Z = mesh.shape["section"], mesh.shape["student"], mesh.shape["dp"]

    def on_device(
        in_flight, segments, norm_gain, w_qkv, w_out, final_gain, student_rows, student_gain, w_head
    ):
        tokens, model = in_flight.shape[2:]
        wid = w_out.shape[1]
        T, share = student_rows.shape[1], tokens // Z
        sw, block = w_head.shape[1:]
        cw, fw = model // Z, sw // Z
        R = 4 if Z <= 4 else 2
        vmem = pl.BlockSpec(memory_space=pltpu.VMEM)
        hbm = pl.BlockSpec(memory_space=pl.ANY)
        dma = pltpu.SemaphoreType.DMA
        K = max(Z - 1, 1)
        adv, grad = pl.pallas_call(
            functools.partial(window_kernel, S, M, Z, T, R),
            out_shape=(
                jax.ShapeDtypeStruct((share, model), BF16),
                jax.ShapeDtypeStruct((fw, block), F32),
            ),
            in_specs=[vmem, vmem, vmem, hbm, hbm, vmem, vmem, vmem, hbm],
            out_specs=(vmem, vmem),
            scratch_shapes=[
                pltpu.VMEM((3, model, wid), BF16),
                pltpu.VMEM((Z * wid, cw), BF16),
                pltpu.VMEM((sw, block), BF16),
                pltpu.VMEM((tokens, model), BF16),
                pltpu.VMEM((T - 1, tokens, model), BF16),
                pltpu.VMEM((T, tokens, Z * wid), BF16),
                pltpu.VMEM((T - 1, tokens, cw), BF16),
                pltpu.VMEM((T, Z, share, cw), BF16),
                pltpu.VMEM((T, share, model), BF16),
                pltpu.VMEM((T, share, model), BF16),
                pltpu.VMEM((T, M, Z, share, block), BF16),
                pltpu.VMEM((share, model), BF16),
                pltpu.VMEM((Z, T, M, share, sw), BF16),
                pltpu.VMEM((Z, T, M, share, block), F32),
                pltpu.VMEM((Z, T, M * share, fw), BF16),
                pltpu.VMEM((Z, M * share, block), BF16),
                dma((3,)),
                dma((K,)), dma((K,)), dma((K,)), dma((K,)),
                dma((T, K)), dma((T, K)),
                dma((T - 1, R)), dma((T - 1, R)),
                dma((T - 1, K, R)), dma((T - 1, K, R)),
                dma((T - 1, K, R)), dma((T - 1, K, R)),
                dma((T, K)), dma((T, K)),
                dma((Z,)), dma((Z,)),
                dma((T, S)), dma((T,)),
                dma((K,)), dma((K,)), dma((S,)), dma((S,)),
                dma((T, K)), dma((T, K)),
                dma((T, M, Z)), dma((T, M, Z)),
            ],
            compiler_params=pltpu.CompilerParams(
                collective_id=0, has_side_effects=True, vmem_limit_bytes=58 << 20
            ),
        )(
            in_flight[0, 0], segments, norm_gain, jnp.transpose(w_qkv[0], (1, 0, 2)), w_out[0],
            final_gain[None], student_rows[0], student_gain, w_head[0],
        )
        return adv[None, None], grad[None]

    in_specs = (
        P("section", "student", None, None),
        P(None, "student", None),
        P("section", None),
        P("section", None, None, "dp"),
        P("section", "dp", None),
        P(),
        P("student", None, None, "dp", None),
        P("student", None),
        P("student", None, "section"),
    )
    out_specs = (P("section", "student", "dp", None), P("student", "dp", "section"))
    return jax.shard_map(
        on_device, mesh=mesh, in_specs=in_specs, out_specs=out_specs, check_vma=False
    )
```

```python
import functools

import jax
import jax.numpy as jnp
from jax import lax
from jax.experimental import pallas as pl
from jax.experimental.pallas import tpu as pltpu
from jax.sharding import PartitionSpec as P

HEAD_SIZE = 128
LN_ROWS = 16
BF16 = jnp.bfloat16
F32 = jnp.float32
MESH = pl.DeviceIdType.MESH


def layer_norm(rows, gain):
    rows = rows.astype(F32)
    centred = rows - jnp.mean(rows, axis=-1, keepdims=True)
    spread = jnp.mean(centred * centred, axis=-1, keepdims=True)
    return centred * lax.rsqrt(spread + 1e-06) * gain


def attend(query, keys, values, same):
    scores = lax.dot_general(
        query, keys, (((1,), (1,)), ((), ())), preferred_element_type=F32
    ) * HEAD_SIZE ** (-0.5)
    scores = jnp.where(same, scores, -1e30)
    top = jnp.max(scores, axis=-1, keepdims=True)
    expo = jnp.exp(scores - top)
    probs = (expo / jnp.sum(expo, axis=-1, keepdims=True)).astype(BF16)
    return jnp.dot(probs, values, preferred_element_type=F32).astype(BF16)


def window_kernel(
    S, M, Z, T, R,
    x_ref, seg_ref, gain_ref, wqkv_ref, wout_ref, fgain_ref, srows_ref, sgain_ref, whead_ref,
    adv_ref, grad_ref,
    wqkv, wofull, whead, normed, xfull, mixfull, xs, xrows, fin, tg, tbuf, advbuf,
    sall, pred, fown, errs,
    local_sem, wo_s, wo_r, wf_s, wf_r, mx_s, mx_r, sh_s, sh_r, ar_s, ar_r, al_s, al_r,
    ro_s, ro_r, ad_s, ad_r, tg_s, tg_r, fe_s, fe_r, fp_s, fp_r,
    er_s, er_r, ml_s, ml_r,
):
    s = lax.axis_index("section")
    c = lax.axis_index("student")
    z = lax.axis_index("dp")
    root = S - 1
    tokens, model = x_ref.shape
    wid = wout_ref.shape[0]
    share = tokens // Z
    cw = model // Z
    block = whead_ref.shape[1]
    sw = whead_ref.shape[0]
    fw = sw // Z
    ow = sw // S
    step_rows = tokens // R
    halves = 2 if M % 2 == 0 else 1
    part = c % halves
    hw = wid // halves
    sends = []

    def remote(src, dst, send, recv, where):
        return pltpu.make_async_remote_copy(
            src_ref=src, dst_ref=dst, send_sem=send, recv_sem=recv,
            device_id=where, device_id_type=MESH,
        )

    def post(cond, build):
        if cond is True:
            build().start()
        else:
            pl.when(cond)(lambda: build().start())
        sends.append((cond, build))

    def zmod(value):
        return lax.rem(value + Z, Z)

    def cols(index):
        return pl.ds(pl.multiple_of(index * cw, 128), cw)

    load_qkv = pltpu.make_async_copy(wqkv_ref, wqkv, local_sem.at[0])
    load_head = pltpu.make_async_copy(whead_ref, whead, local_sem.at[1])
    own_wo = pltpu.make_async_copy(
        wout_ref.at[:, cols(z)],
        wofull.at[pl.ds(pl.multiple_of(z * wid, wid), wid), :],
        local_sem.at[2],
    )
    load_qkv.start()
    own_wo.start()
    load_head.start()

    barrier = pltpu.get_barrier_semaphore()

    def greet(where):
        pl.semaphore_signal(barrier, inc=1, device_id=where, device_id_type=MESH)

    for k in range(1, Z):
        greet((s, c, zmod(z + k)))
    for k in range(Z):
        pl.when(s > 0)(functools.partial(greet, (s - 1, c, zmod(z + k))))
        pl.when(s < root)(functools.partial(greet, (s + 1, c, zmod(z + k))))
    for at in range(S):
        far = jnp.logical_or(s - at > 1, at - s > 1)
        pl.when(far)(functools.partial(greet, (jnp.int32(at), c, z)))
        for dm in range(1, M):
            greet((jnp.int32(at), lax.rem(c + dm, M), z))
    for at in range(S):
        near = min(at, 1) + min(root - at, 1)
        peers = (Z - 1) + Z * near + (S - 1 - near) + S * (M - 1)
        pl.when(s == at)(functools.partial(pl.semaphore_wait, barrier, peers))

    def wo_rows(source, which):
        return pl.ds(pl.multiple_of(source * wid + which * hw, hw), hw)

    for k in sorted(range(1, Z), reverse=True):
        def build(k=k):
            to = zmod(z + k)
            return remote(
                wout_ref.at[pl.ds(pl.multiple_of(part * hw, hw), hw), cols(to)],
                wofull.at[wo_rows(z, part), :],
                wo_s.at[k - 1], wo_r.at[k - 1], (s, c, to),
            )
        post(True, build)

    def pass_on(k):
        source = zmod(z - k)
        mine = wofull.at[wo_rows(source, part), :]
        mate = c + 1 - 2 * part
        return remote(mine, mine, wf_s.at[k - 1], wf_r.at[k - 1], (s, mate, z))

    def gather_wo():
        for k in range(1, Z):
            source = zmod(z - k)
            mine = wofull.at[wo_rows(source, part), :]
            remote(mine, mine, wo_s.at[k - 1], wo_r.at[k - 1], (s, c, source)).wait_recv()
            if halves == 2:
                post(True, functools.partial(pass_on, k))
        if halves == 2:
            for k in range(1, Z):
                source = zmod(z - k)
                other = wofull.at[wo_rows(source, 1 - part), :]
                remote(other, other, wf_s.at[k - 1], wf_r.at[k - 1],
                       (s, c + 1 - 2 * part, z)).wait_recv()
        own_wo.wait()

    def scols(index):
        return pl.ds(pl.multiple_of(index * ow, 128), ow)

    def spread_rows():
        sall[0] = srows_ref[...]
        for k in range(1, Z):
            def build(k=k):
                return remote(srows_ref.at[:, :, :, scols(s)], sall.at[k, :, :, :, scols(s)],
                              fe_s.at[k - 1], fe_r.at[k - 1], (s, c, zmod(z + k)))
            post(True, build)

    def pass_rows():
        for k in range(1, Z):
            there = sall.at[k, :, :, :, scols(s)]
            remote(there, there, fe_s.at[k - 1], fe_r.at[k - 1], (s, c, zmod(z - k))).wait_recv()
        for k in range(1, S):
            def build(k=k):
                there = sall.at[pl.ds(1, Z - 1), :, :, :, scols(s)]
                return remote(there, there, fp_s.at[k - 1], fp_r.at[k - 1],
                              (lax.rem(s + k, S), c, z))
            post(True, build)

    def take_rows():
        for k in range(1, S):
            where = lax.rem(s + S - k, S)
            there = sall.at[pl.ds(1, Z - 1), :, :, :, scols(where)]
            remote(there, there, fp_s.at[k - 1], fp_r.at[k - 1], (where, c, z)).wait_recv()
        load_head.wait()

    def student(low, high):
        def one(k, carry):
            rows = layer_norm(sall[k].astype(F32).reshape(T * M * share, sw), sgain_ref[...])
            rows = rows.astype(BF16)
            for zz in range(Z):
                def own(zz=zz):
                    fown[k] = rows[:, zz * fw:(zz + 1) * fw].reshape(T, M * share, fw)
                pl.when(z == zz)(own)
            pred[k] = jnp.dot(rows, whead[...], preferred_element_type=F32).reshape(
                T, M, share, block
            )
            return carry

        lax.fori_loop(low, high, one, 0)

    def spread(t):
        def take():
            there = tbuf.at[t, c, 0]
            remote(there, there, tg_s.at[t, 0], tg_r.at[t], (root, c, z)).wait_recv()
        pl.when(s != root)(take)
        for k in range(1, Z):
            def build(k=k):
                return remote(tbuf.at[t, c, 0], tbuf.at[t, c, k], er_s.at[t, k - 1],
                              er_r.at[t, k - 1], (s, c, zmod(z + k)))
            post(True, build)

    def relay(t):
        for k in range(Z):
            there = tbuf.at[t, c, k]
            if k:
                remote(there, there, er_s.at[t, k - 1], er_r.at[t, k - 1],
                       (s, c, zmod(z - k))).wait_recv()
            for dm in range(1, M):
                def build(k=k, dm=dm):
                    there = tbuf.at[t, c, k]
                    return remote(there, there, ml_s.at[t, dm - 1, k], ml_r.at[t, dm - 1, k],
                                  (s, lax.rem(c + dm, M), z))
                post(True, build)

    def gradient(t):
        for dm in range(1, M):
            for k in range(Z):
                who = lax.rem(c + M - dm, M)
                there = tbuf.at[t, who, k]
                remote(there, there, ml_s.at[t, dm - 1, k], ml_r.at[t, dm - 1, k],
                       (s, who, z)).wait_recv()

        def one(k, carry):
            err = (pred[k, t] - tbuf[t, :, k].astype(F32)) * (2.0 / tokens)
            errs[k] = err.reshape(M * share, block).astype(BF16)
            return carry

        lax.fori_loop(0, Z, one, 0)
        term = lax.dot_general(
            fown[:, t].reshape(Z * M * share, fw), errs[...].reshape(Z * M * share, block),
            (((0,), (0,)), ((), ())), preferred_element_type=F32,
        )
        if t == 0:
            grad_ref[...] = term
        else:
            grad_ref[...] += term

    def gather_state(t, active, between):
        def piece(r, origin):
            return xfull.at[t - 1, pl.ds(r * step_rows, step_rows), cols(origin)]

        def to_right(r, k):
            there = piece(r, z - k)
            return remote(there, there, ar_s.at[t - 1, k, r], ar_r.at[t - 1, k, r], (s, c, z + 1))

        def to_left(r, k):
            there = piece(r, z + k)
            return remote(there, there, al_s.at[t - 1, k, r], al_r.at[t - 1, k, r], (s, c, z - 1))

        def right_from(r, k):
            there = piece(r, z - k)
            remote(there, there, ar_s.at[t - 1, k - 1, r], ar_r.at[t - 1, k - 1, r],
                   (s, c, z - 1)).wait_recv()

        def left_from(r, k):
            there = piece(r, z + k)
            remote(there, there, al_s.at[t - 1, k - 1, r], al_r.at[t - 1, k - 1, r],
                   (s, c, z + 1)).wait_recv()

        for r in range(R):
            def first(r=r):
                there = piece(r, z)
                remote(there, there, sh_s.at[t - 1, r], sh_r.at[t - 1, r],
                       (s - 1, c, z)).wait_recv()
            pl.when(active)(first)
            post(jnp.logical_and(active, z < Z - 1), functools.partial(to_right, r, 0))
            post(jnp.logical_and(active, z > 0), functools.partial(to_left, r, 0))
        between()
        for k in range(1, Z):
            for r in range(R):
                pl.when(jnp.logical_and(active, z >= k))(functools.partial(right_from, r, k))
                if k < Z - 1:
                    post(jnp.logical_and(active, jnp.logical_and(z >= k, z < Z - 1)),
                         functools.partial(to_right, r, k))
                pl.when(jnp.logical_and(active, z + k < Z))(functools.partial(left_from, r, k))
                if k < Z - 1:
                    post(jnp.logical_and(active, jnp.logical_and(z + k < Z, z > 0)),
                         functools.partial(to_left, r, k))

    def mix_cols(index):
        return pl.ds(pl.multiple_of(index * wid, 128), wid)

    def mixing(t):
        source = x_ref if t == 0 else xfull.at[t - 1]

        def norm_rows(i, carry):
            rows = pl.ds(pl.multiple_of(i * LN_ROWS, LN_ROWS), LN_ROWS)
            normed[rows, :] = layer_norm(source[rows, :], gain_ref[...]).astype(BF16)
            return carry

        lax.fori_loop(0, tokens // LN_ROWS, norm_rows, 0)
        if t == 0:
            load_qkv.wait()
        rows = normed[...]
        query, keys, values = [
            jnp.dot(rows, wqkv[j], preferred_element_type=F32).astype(BF16)
            for j in range(3)
        ]
        crops = jnp.broadcast_to(seg_ref[s - t].astype(F32), (tokens, tokens))
        same = crops == crops.T
        outs = []
        for h in range(wid // HEAD_SIZE):
            at = slice(h * HEAD_SIZE, (h + 1) * HEAD_SIZE)
            outs.append(attend(query[:, at], keys[:, at], values[:, at], same))
        mixfull[t, :, mix_cols(z)] = jnp.concatenate(outs, axis=1)

    def send_mixed(t, active):
        for k in range(1, Z):
            def build(k=k):
                own = mixfull.at[t, :, mix_cols(z)]
                return remote(own, own, mx_s.at[t, k - 1], mx_r.at[t, k - 1],
                              (s, c, zmod(z + k)))
            post(active, build)

    def project(t):
        for k in range(1, Z):
            there = mixfull.at[t, :, mix_cols(zmod(z - k))]
            remote(there, there, mx_s.at[t, k - 1], mx_r.at[t, k - 1],
                   (s, c, zmod(z - k))).wait_recv()
        own = x_ref[:, cols(z)] if t == 0 else xfull[t - 1, :, cols(z)]
        summed = own.astype(F32) + jnp.dot(mixfull[t], wofull[...], preferred_element_type=F32)
        if t < T - 1:
            xs[t] = summed.astype(BF16)
        xrows[t] = summed.reshape(Z, share, cw).astype(BF16)

    def send_state(t, active):
        if t < T - 1:
            for r in range(R):
                def build(r=r):
                    at = pl.ds(r * step_rows, step_rows)
                    return remote(xs.at[t, at, :], xfull.at[t, at, cols(z)],
                                  sh_s.at[t, r], sh_r.at[t, r], (s + 1, c, z))
                post(jnp.logical_and(active, s < root), build)
        else:
            for k in range(Z):
                def build(k=k):
                    to = zmod(z + k)
                    return remote(xrows.at[t, to], advbuf.at[:, cols(z)],
                                  ad_s.at[k], ad_r.at[k], (s + 1, c, to))
                post(jnp.logical_and(active, s < root), build)
        for k in range(1, Z):
            def build_row(k=k):
                to = zmod(z + k)
                return remote(xrows.at[t, to], fin.at[t, :, cols(z)],
                              ro_s.at[t, k - 1], ro_r.at[t, k - 1], (s, c, to))
            post(s == root, build_row)

    def finish(t):
        def rows():
            fin[t, :, cols(z)] = xrows[t, z]
            for k in range(1, Z):
                there = fin.at[t, :, cols(zmod(z - k))]
                remote(there, there, ro_s.at[t, k - 1], ro_r.at[t, k - 1],
                       (s, c, zmod(z - k))).wait_recv()
            tg[t] = layer_norm(fin[t], fgain_ref[...]).astype(BF16)
            tbuf[t, c, 0] = tg[t, :, root * block:(root + 1) * block]

        pl.when(s == root)(rows)
        for to in range(root):
            def build(to=to):
                return remote(tg.at[t, :, to * block:(to + 1) * block], tbuf.at[t, c, 0],
                              tg_s.at[t, to], tg_r.at[t], (jnp.int32(to), c, z))
            post(s == root, build)

    for t in range(T):
        active = True if t == 0 else s >= t
        if t == 0:
            mixing(0)
        else:
            def between(t=t):
                finish(t - 1)
                if t == 1:
                    pass_rows()

            gather_state(t, active, between)
            if t > 1:
                relay(t - 2)
                spread(t - 1)
            pl.when(active)(functools.partial(mixing, t))
        send_mixed(t, active)
        if t == 0:
            spread_rows()
            gather_wo()
            project(0)
        else:
            if t == 1:
                spread(0)
                take_rows()
                student(0, Z // 2)
            if t == T - 1:
                relay(t - 1)
                student(Z // 2, Z)
            pl.when(active)(functools.partial(project, t))
        send_state(t, active)
        if t == T - 1:
            for before in range(t):
                gradient(before)

    finish(T - 1)
    spread(T - 1)
    relay(T - 1)
    gradient(T - 1)

    def arrived():
        for k in range(Z):
            there = advbuf.at[:, cols(zmod(z - k))]
            remote(there, there, ad_s.at[k], ad_r.at[k], (s - 1, c, zmod(z - k))).wait_recv()
        adv_ref[...] = advbuf[...]

    def nothing():
        adv_ref[...] = jnp.zeros_like(adv_ref)

    pl.when(s >= T)(arrived)
    pl.when(s < T)(nothing)
    for cond, build in sends:
        if cond is True:
            build().wait_send()
        else:
            pl.when(cond)(lambda build=build: build().wait_send())


def solution(mesh):
    S, M, Z = mesh.shape["section"], mesh.shape["student"], mesh.shape["dp"]

    def on_device(
        in_flight, segments, norm_gain, w_qkv, w_out, final_gain, student_rows, student_gain, w_head
    ):
        tokens, model = in_flight.shape[2:]
        wid = w_out.shape[1]
        T, share = student_rows.shape[1], tokens // Z
        sw, block = w_head.shape[1:]
        cw, fw = model // Z, sw // Z
        R = 4 if Z <= 4 else 2
        vmem = pl.BlockSpec(memory_space=pltpu.VMEM)
        hbm = pl.BlockSpec(memory_space=pl.ANY)
        dma = pltpu.SemaphoreType.DMA
        K = max(Z - 1, 1)
        adv, grad = pl.pallas_call(
            functools.partial(window_kernel, S, M, Z, T, R),
            out_shape=(
                jax.ShapeDtypeStruct((share, model), BF16),
                jax.ShapeDtypeStruct((fw, block), F32),
            ),
            in_specs=[vmem, vmem, vmem, hbm, hbm, vmem, vmem, vmem, hbm],
            out_specs=(vmem, vmem),
            scratch_shapes=[
                pltpu.VMEM((3, model, wid), BF16),
                pltpu.VMEM((Z * wid, cw), BF16),
                pltpu.VMEM((sw, block), BF16),
                pltpu.VMEM((tokens, model), BF16),
                pltpu.VMEM((T - 1, tokens, model), BF16),
                pltpu.VMEM((T, tokens, Z * wid), BF16),
                pltpu.VMEM((T - 1, tokens, cw), BF16),
                pltpu.VMEM((T, Z, share, cw), BF16),
                pltpu.VMEM((T, share, model), BF16),
                pltpu.VMEM((T, share, model), BF16),
                pltpu.VMEM((T, M, Z, share, block), BF16),
                pltpu.VMEM((share, model), BF16),
                pltpu.VMEM((Z, T, M, share, sw), BF16),
                pltpu.VMEM((Z, T, M, share, block), F32),
                pltpu.VMEM((Z, T, M * share, fw), BF16),
                pltpu.VMEM((Z, M * share, block), BF16),
                dma((3,)),
                dma((K,)), dma((K,)), dma((K,)), dma((K,)),
                dma((T, K)), dma((T, K)),
                dma((T - 1, R)), dma((T - 1, R)),
                dma((T - 1, K, R)), dma((T - 1, K, R)),
                dma((T - 1, K, R)), dma((T - 1, K, R)),
                dma((T, K)), dma((T, K)),
                dma((Z,)), dma((Z,)),
                dma((T, S)), dma((T,)),
                dma((K,)), dma((K,)), dma((S,)), dma((S,)),
                dma((T, K)), dma((T, K)),
                dma((T, M, Z)), dma((T, M, Z)),
            ],
            compiler_params=pltpu.CompilerParams(
                collective_id=0, has_side_effects=True, vmem_limit_bytes=58 << 20
            ),
        )(
            in_flight[0, 0], segments, norm_gain, jnp.transpose(w_qkv[0], (1, 0, 2)), w_out[0],
            final_gain[None], student_rows[0], student_gain, w_head[0],
        )
        return adv[None, None], grad[None]

    in_specs = (
        P("section", "student", None, None),
        P(None, "student", None),
        P("section", None),
        P("section", None, None, "dp"),
        P("section", "dp", None),
        P(),
        P("student", None, None, "dp", None),
        P("student", None),
        P("student", None, "section"),
    )
    out_specs = (P("section", "student", "dp", None), P("student", "dp", "section"))
    return jax.shard_map(
        on_device, mesh=mesh, in_specs=in_specs, out_specs=out_specs, check_vma=False
    )
```

```python
import functools

import jax
import jax.numpy as jnp
from jax import lax
from jax.experimental import pallas as pl
from jax.experimental.pallas import tpu as pltpu
from jax.sharding import PartitionSpec as P

HEAD_SIZE = 128
LN_ROWS = 16
BF16 = jnp.bfloat16
F32 = jnp.float32
MESH = pl.DeviceIdType.MESH


def layer_norm(rows, gain):
    rows = rows.astype(F32)
    centred = rows - jnp.mean(rows, axis=-1, keepdims=True)
    spread = jnp.mean(centred * centred, axis=-1, keepdims=True)
    return centred * lax.rsqrt(spread + 1e-06) * gain


def attend(query, keys, values, same):
    scores = lax.dot_general(
        query, keys, (((1,), (1,)), ((), ())), preferred_element_type=F32
    ) * HEAD_SIZE ** (-0.5)
    scores = jnp.where(same, scores, -1e30)
    top = jnp.max(scores, axis=-1, keepdims=True)
    expo = jnp.exp(scores - top)
    probs = (expo / jnp.sum(expo, axis=-1, keepdims=True)).astype(BF16)
    return jnp.dot(probs, values, preferred_element_type=F32).astype(BF16)


def window_kernel(
    S, M, Z, T, R,
    x_ref, seg_ref, gain_ref, wqkv_ref, wout_ref, fgain_ref, srows_ref, sgain_ref, whead_ref,
    adv_ref, grad_ref,
    wqkv, wofull, whead, normed, xfull, mixfull, xs, xrows, fin, tg, tbuf, advbuf,
    sall, pred, fown, errs,
    local_sem, wo_s, wo_r, wf_s, wf_r, mx_s, mx_r, sh_s, sh_r, ar_s, ar_r, al_s, al_r,
    ro_s, ro_r, ad_s, ad_r, tg_s, tg_r, fe_s, fe_r, fp_s, fp_r,
    er_s, er_r, ml_s, ml_r,
):
    s = lax.axis_index("section")
    c = lax.axis_index("student")
    z = lax.axis_index("dp")
    root = S - 1
    tokens, model = x_ref.shape
    wid = wout_ref.shape[0]
    share = tokens // Z
    cw = model // Z
    block = whead_ref.shape[1]
    sw = whead_ref.shape[0]
    fw = sw // Z
    ow = sw // S
    step_rows = tokens // R
    halves = 2 if M % 2 == 0 else 1
    part = c % halves
    hw = wid // halves
    sends = []

    def remote(src, dst, send, recv, where):
        return pltpu.make_async_remote_copy(
            src_ref=src, dst_ref=dst, send_sem=send, recv_sem=recv,
            device_id=where, device_id_type=MESH,
        )

    def post(cond, build):
        if cond is True:
            build().start()
        else:
            pl.when(cond)(lambda: build().start())
        sends.append((cond, build))

    def zmod(value):
        return lax.rem(value + Z, Z)

    def cols(index):
        return pl.ds(pl.multiple_of(index * cw, 128), cw)

    load_qkv = pltpu.make_async_copy(wqkv_ref, wqkv, local_sem.at[0])
    load_head = pltpu.make_async_copy(whead_ref, whead, local_sem.at[1])
    own_wo = pltpu.make_async_copy(
        wout_ref.at[:, cols(z)],
        wofull.at[pl.ds(pl.multiple_of(z * wid, wid), wid), :],
        local_sem.at[2],
    )
    load_qkv.start()
    own_wo.start()
    load_head.start()

    barrier = pltpu.get_barrier_semaphore()

    def greet(where):
        pl.semaphore_signal(barrier, inc=1, device_id=where, device_id_type=MESH)

    for k in range(1, Z):
        greet((s, c, zmod(z + k)))
    for k in range(Z):
        pl.when(s > 0)(functools.partial(greet, (s - 1, c, zmod(z + k))))
        pl.when(s < root)(functools.partial(greet, (s + 1, c, zmod(z + k))))
    for at in range(S):
        far = jnp.logical_or(s - at > 1, at - s > 1)
        pl.when(far)(functools.partial(greet, (jnp.int32(at), c, z)))
        for dm in range(1, M):
            greet((jnp.int32(at), lax.rem(c + dm, M), z))
    for at in range(S):
        near = min(at, 1) + min(root - at, 1)
        peers = (Z - 1) + Z * near + (S - 1 - near) + S * (M - 1)
        pl.when(s == at)(functools.partial(pl.semaphore_wait, barrier, peers))

    def wo_rows(source, which):
        return pl.ds(pl.multiple_of(source * wid + which * hw, hw), hw)

    for k in sorted(range(1, Z), reverse=True):
        def build(k=k):
            to = zmod(z + k)
            return remote(
                wout_ref.at[pl.ds(pl.multiple_of(part * hw, hw), hw), cols(to)],
                wofull.at[wo_rows(z, part), :],
                wo_s.at[k - 1], wo_r.at[k - 1], (s, c, to),
            )
        post(True, build)

    def pass_on(k):
        source = zmod(z - k)
        mine = wofull.at[wo_rows(source, part), :]
        mate = c + 1 - 2 * part
        return remote(mine, mine, wf_s.at[k - 1], wf_r.at[k - 1], (s, mate, z))

    def gather_wo():
        for k in range(1, Z):
            source = zmod(z - k)
            mine = wofull.at[wo_rows(source, part), :]
            remote(mine, mine, wo_s.at[k - 1], wo_r.at[k - 1], (s, c, source)).wait_recv()
            if halves == 2:
                post(True, functools.partial(pass_on, k))
        if halves == 2:
            for k in range(1, Z):
                source = zmod(z - k)
                other = wofull.at[wo_rows(source, 1 - part), :]
                remote(other, other, wf_s.at[k - 1], wf_r.at[k - 1],
                       (s, c + 1 - 2 * part, z)).wait_recv()
        own_wo.wait()

    def scols(index):
        return pl.ds(pl.multiple_of(index * ow, 128), ow)

    def spread_rows():
        sall[0] = srows_ref[...]
        for k in range(1, Z):
            def build(k=k):
                return remote(srows_ref.at[:, :, :, scols(s)], sall.at[k, :, :, :, scols(s)],
                              fe_s.at[k - 1], fe_r.at[k - 1], (s, c, zmod(z + k)))
            post(True, build)

    def pass_rows():
        for k in range(1, Z):
            there = sall.at[k, :, :, :, scols(s)]
            remote(there, there, fe_s.at[k - 1], fe_r.at[k - 1], (s, c, zmod(z - k))).wait_recv()
        for k in range(1, S):
            def build(k=k):
                there = sall.at[pl.ds(1, Z - 1), :, :, :, scols(s)]
                return remote(there, there, fp_s.at[k - 1], fp_r.at[k - 1],
                              (lax.rem(s + k, S), c, z))
            post(True, build)

    def take_rows():
        for k in range(1, S):
            where = lax.rem(s + S - k, S)
            there = sall.at[pl.ds(1, Z - 1), :, :, :, scols(where)]
            remote(there, there, fp_s.at[k - 1], fp_r.at[k - 1], (where, c, z)).wait_recv()
        load_head.wait()

    def student(low, high):
        def one(k, carry):
            rows = layer_norm(sall[k].astype(F32).reshape(T * M * share, sw), sgain_ref[...])
            rows = rows.astype(BF16)
            for zz in range(Z):
                def own(zz=zz):
                    fown[k] = rows[:, zz * fw:(zz + 1) * fw].reshape(T, M * share, fw)
                pl.when(z == zz)(own)
            pred[k] = jnp.dot(rows, whead[...], preferred_element_type=F32).reshape(
                T, M, share, block
            )
            return carry

        lax.fori_loop(low, high, one, 0)

    def spread(t):
        def take():
            there = tbuf.at[t, c, 0]
            remote(there, there, tg_s.at[t, 0], tg_r.at[t], (root, c, z)).wait_recv()
        pl.when(s != root)(take)
        for k in range(1, Z):
            def build(k=k):
                return remote(tbuf.at[t, c, 0], tbuf.at[t, c, k], er_s.at[t, k - 1],
                              er_r.at[t, k - 1], (s, c, zmod(z + k)))
            post(True, build)

    def relay(t):
        for k in range(Z):
            there = tbuf.at[t, c, k]
            if k:
                remote(there, there, er_s.at[t, k - 1], er_r.at[t, k - 1],
                       (s, c, zmod(z - k))).wait_recv()
            for dm in range(1, M):
                def build(k=k, dm=dm):
                    there = tbuf.at[t, c, k]
                    return remote(there, there, ml_s.at[t, dm - 1, k], ml_r.at[t, dm - 1, k],
                                  (s, lax.rem(c + dm, M), z))
                post(True, build)

    def gradient(t):
        for dm in range(1, M):
            for k in range(Z):
                who = lax.rem(c + M - dm, M)
                there = tbuf.at[t, who, k]
                remote(there, there, ml_s.at[t, dm - 1, k], ml_r.at[t, dm - 1, k],
                       (s, who, z)).wait_recv()

        def one(k, carry):
            err = (pred[k, t] - tbuf[t, :, k].astype(F32)) * (2.0 / tokens)
            errs[k] = err.reshape(M * share, block).astype(BF16)
            return carry

        lax.fori_loop(0, Z, one, 0)
        term = lax.dot_general(
            fown[:, t].reshape(Z * M * share, fw), errs[...].reshape(Z * M * share, block),
            (((0,), (0,)), ((), ())), preferred_element_type=F32,
        )
        if t == 0:
            grad_ref[...] = term
        else:
            grad_ref[...] += term

    def gather_state(t, active, between):
        def piece(r, origin):
            return xfull.at[t - 1, pl.ds(r * step_rows, step_rows), cols(origin)]

        def to_right(r, k):
            there = piece(r, z - k)
            return remote(there, there, ar_s.at[t - 1, k, r], ar_r.at[t - 1, k, r], (s, c, z + 1))

        def to_left(r, k):
            there = piece(r, z + k)
            return remote(there, there, al_s.at[t - 1, k, r], al_r.at[t - 1, k, r], (s, c, z - 1))

        def right_from(r, k):
            there = piece(r, z - k)
            remote(there, there, ar_s.at[t - 1, k - 1, r], ar_r.at[t - 1, k - 1, r],
                   (s, c, z - 1)).wait_recv()

        def left_from(r, k):
            there = piece(r, z + k)
            remote(there, there, al_s.at[t - 1, k - 1, r], al_r.at[t - 1, k - 1, r],
                   (s, c, z + 1)).wait_recv()

        for r in range(R):
            def first(r=r):
                there = piece(r, z)
                remote(there, there, sh_s.at[t - 1, r], sh_r.at[t - 1, r],
                       (s - 1, c, z)).wait_recv()
            pl.when(active)(first)
            post(jnp.logical_and(active, z < Z - 1), functools.partial(to_right, r, 0))
            post(jnp.logical_and(active, z > 0), functools.partial(to_left, r, 0))
        between()
        for k in range(1, Z):
            for r in range(R):
                pl.when(jnp.logical_and(active, z >= k))(functools.partial(right_from, r, k))
                if k < Z - 1:
                    post(jnp.logical_and(active, jnp.logical_and(z >= k, z < Z - 1)),
                         functools.partial(to_right, r, k))
                pl.when(jnp.logical_and(active, z + k < Z))(functools.partial(left_from, r, k))
                if k < Z - 1:
                    post(jnp.logical_and(active, jnp.logical_and(z + k < Z, z > 0)),
                         functools.partial(to_left, r, k))

    def mix_cols(index):
        return pl.ds(pl.multiple_of(index * wid, 128), wid)

    def mixing(t):
        source = x_ref if t == 0 else xfull.at[t - 1]

        def norm_rows(i, carry):
            rows = pl.ds(pl.multiple_of(i * LN_ROWS, LN_ROWS), LN_ROWS)
            normed[rows, :] = layer_norm(source[rows, :], gain_ref[...]).astype(BF16)
            return carry

        lax.fori_loop(0, tokens // LN_ROWS, norm_rows, 0)
        if t == 0:
            load_qkv.wait()
        rows = normed[...]
        query, keys, values = [
            jnp.dot(rows, wqkv[j], preferred_element_type=F32).astype(BF16)
            for j in range(3)
        ]
        crops = jnp.broadcast_to(seg_ref[s - t].astype(F32), (tokens, tokens))
        same = crops == crops.T
        outs = []
        for h in range(wid // HEAD_SIZE):
            at = slice(h * HEAD_SIZE, (h + 1) * HEAD_SIZE)
            outs.append(attend(query[:, at], keys[:, at], values[:, at], same))
        mixfull[t, :, mix_cols(z)] = jnp.concatenate(outs, axis=1)

    def send_mixed(t, active):
        for k in range(1, Z):
            def build(k=k):
                own = mixfull.at[t, :, mix_cols(z)]
                return remote(own, own, mx_s.at[t, k - 1], mx_r.at[t, k - 1],
                              (s, c, zmod(z + k)))
            post(active, build)

    def project(t):
        for k in range(1, Z):
            there = mixfull.at[t, :, mix_cols(zmod(z - k))]
            remote(there, there, mx_s.at[t, k - 1], mx_r.at[t, k - 1],
                   (s, c, zmod(z - k))).wait_recv()
        own = x_ref[:, cols(z)] if t == 0 else xfull[t - 1, :, cols(z)]
        summed = own.astype(F32) + jnp.dot(mixfull[t], wofull[...], preferred_element_type=F32)
        if t < T - 1:
            xs[t] = summed.astype(BF16)
        xrows[t] = summed.reshape(Z, share, cw).astype(BF16)

    def send_state(t, active):
        if t < T - 1:
            for r in range(R):
                def build(r=r):
                    at = pl.ds(r * step_rows, step_rows)
                    return remote(xs.at[t, at, :], xfull.at[t, at, cols(z)],
                                  sh_s.at[t, r], sh_r.at[t, r], (s + 1, c, z))
                post(jnp.logical_and(active, s < root), build)
        else:
            for k in range(Z):
                def build(k=k):
                    to = zmod(z + k)
                    return remote(xrows.at[t, to], advbuf.at[:, cols(z)],
                                  ad_s.at[k], ad_r.at[k], (s + 1, c, to))
                post(jnp.logical_and(active, s < root), build)
        for k in range(1, Z):
            def build_row(k=k):
                to = zmod(z + k)
                return remote(xrows.at[t, to], fin.at[t, :, cols(z)],
                              ro_s.at[t, k - 1], ro_r.at[t, k - 1], (s, c, to))
            post(s == root, build_row)

    def finish(t):
        def rows():
            fin[t, :, cols(z)] = xrows[t, z]
            for k in range(1, Z):
                there = fin.at[t, :, cols(zmod(z - k))]
                remote(there, there, ro_s.at[t, k - 1], ro_r.at[t, k - 1],
                       (s, c, zmod(z - k))).wait_recv()
            tg[t] = layer_norm(fin[t], fgain_ref[...]).astype(BF16)
            tbuf[t, c, 0] = tg[t, :, root * block:(root + 1) * block]

        pl.when(s == root)(rows)
        for to in range(root):
            def build(to=to):
                return remote(tg.at[t, :, to * block:(to + 1) * block], tbuf.at[t, c, 0],
                              tg_s.at[t, to], tg_r.at[t], (jnp.int32(to), c, z))
            post(s == root, build)

    for t in range(T):
        active = True if t == 0 else s >= t
        if t == 0:
            mixing(0)
        else:
            gather_state(t, active, functools.partial(finish, t - 1))
            if t == 1:
                pass_rows()
            else:
                relay(t - 2)
                spread(t - 1)
            pl.when(active)(functools.partial(mixing, t))
        send_mixed(t, active)
        if t == 0:
            spread_rows()
            gather_wo()
            project(0)
        else:
            if t == 1:
                spread(0)
            if t == T - 1:
                relay(t - 1)
                take_rows()
                student(0, Z)
            pl.when(active)(functools.partial(project, t))
        send_state(t, active)
        if t == T - 1:
            for before in range(t):
                gradient(before)

    finish(T - 1)
    spread(T - 1)
    relay(T - 1)
    gradient(T - 1)

    def arrived():
        for k in range(Z):
            there = advbuf.at[:, cols(zmod(z - k))]
            remote(there, there, ad_s.at[k], ad_r.at[k], (s - 1, c, zmod(z - k))).wait_recv()
        adv_ref[...] = advbuf[...]

    def nothing():
        adv_ref[...] = jnp.zeros_like(adv_ref)

    pl.when(s >= T)(arrived)
    pl.when(s < T)(nothing)
    for cond, build in sends:
        if cond is True:
            build().wait_send()
        else:
            pl.when(cond)(lambda build=build: build().wait_send())


def solution(mesh):
    S, M, Z = mesh.shape["section"], mesh.shape["student"], mesh.shape["dp"]

    def on_device(
        in_flight, segments, norm_gain, w_qkv, w_out, final_gain, student_rows, student_gain, w_head
    ):
        tokens, model = in_flight.shape[2:]
        wid = w_out.shape[1]
        T, share = student_rows.shape[1], tokens // Z
        sw, block = w_head.shape[1:]
        cw, fw = model // Z, sw // Z
        R = 4 if Z <= 4 else 2
        vmem = pl.BlockSpec(memory_space=pltpu.VMEM)
        hbm = pl.BlockSpec(memory_space=pl.ANY)
        dma = pltpu.SemaphoreType.DMA
        K = max(Z - 1, 1)
        adv, grad = pl.pallas_call(
            functools.partial(window_kernel, S, M, Z, T, R),
            out_shape=(
                jax.ShapeDtypeStruct((share, model), BF16),
                jax.ShapeDtypeStruct((fw, block), F32),
            ),
            in_specs=[vmem, vmem, vmem, hbm, hbm, vmem, vmem, vmem, hbm],
            out_specs=(vmem, vmem),
            scratch_shapes=[
                pltpu.VMEM((3, model, wid), BF16),
                pltpu.VMEM((Z * wid, cw), BF16),
                pltpu.VMEM((sw, block), BF16),
                pltpu.VMEM((tokens, model), BF16),
                pltpu.VMEM((T - 1, tokens, model), BF16),
                pltpu.VMEM((T, tokens, Z * wid), BF16),
                pltpu.VMEM((T - 1, tokens, cw), BF16),
                pltpu.VMEM((T, Z, share, cw), BF16),
                pltpu.VMEM((T, share, model), BF16),
                pltpu.VMEM((T, share, model), BF16),
                pltpu.VMEM((T, M, Z, share, block), BF16),
                pltpu.VMEM((share, model), BF16),
                pltpu.VMEM((Z, T, M, share, sw), BF16),
                pltpu.VMEM((Z, T, M, share, block), F32),
                pltpu.VMEM((Z, T, M * share, fw), BF16),
                pltpu.VMEM((Z, M * share, block), BF16),
                dma((3,)),
                dma((K,)), dma((K,)), dma((K,)), dma((K,)),
                dma((T, K)), dma((T, K)),
                dma((T - 1, R)), dma((T - 1, R)),
                dma((T - 1, K, R)), dma((T - 1, K, R)),
                dma((T - 1, K, R)), dma((T - 1, K, R)),
                dma((T, K)), dma((T, K)),
                dma((Z,)), dma((Z,)),
                dma((T, S)), dma((T,)),
                dma((K,)), dma((K,)), dma((S,)), dma((S,)),
                dma((T, K)), dma((T, K)),
                dma((T, M, Z)), dma((T, M, Z)),
            ],
            compiler_params=pltpu.CompilerParams(
                collective_id=0, has_side_effects=True, vmem_limit_bytes=58 << 20
            ),
        )(
            in_flight[0, 0], segments, norm_gain, jnp.transpose(w_qkv[0], (1, 0, 2)), w_out[0],
            final_gain[None], student_rows[0], student_gain, w_head[0],
        )
        return adv[None, None], grad[None]

    in_specs = (
        P("section", "student", None, None),
        P(None, "student", None),
        P("section", None),
        P("section", None, None, "dp"),
        P("section", "dp", None),
        P(),
        P("student", None, None, "dp", None),
        P("student", None),
        P("student", None, "section"),
    )
    out_specs = (P("section", "student", "dp", None), P("student", "dp", "section"))
    return jax.shard_map(
        on_device, mesh=mesh, in_specs=in_specs, out_specs=out_specs, check_vma=False
    )
```
